32 devices in a mesh: dp: 2 (over x), row: 4 (over y, core), col: 4 (over z).
Axes of the slice: x: 2, y: 2, z: 4, core: 2. Of those that a mesh axis runs over, the one named last changes fastest.
Arguments:
- block_input: bfloat16 [8192, 1024], P(('dp', 'row'), 'col'), may hold values from -6 to 6
- norm_attn: bfloat16 [1024], P('col'), may hold values from 0.5 to 1.5
- w_query: bfloat16 [1024, 512], P('col', 'row'), may hold values from -1 to 1, as said below
- w_key: bfloat16 [1024, 512], P('col', 'row'), may hold values from -1 to 1, as said below
- w_value: bfloat16 [1024, 1024], P('col', 'row'), may hold values from -0.1875 to 0.1875
- w_gate_out: bfloat16 [1024, 1024], P('col', 'row'), may hold values from -0.1875 to 0.1875
- w_rank_in: bfloat16 [1024, 16], P('col'), may hold values from -0.1875 to 0.1875
- w_rank_out: bfloat16 [16, 512], P(None, 'row'), may hold values from -1.5 to 1.5
- rank_bias: bfloat16 [512], P('row'), may hold values from 0.5 to 6
- head_gain: bfloat16 [256], replicated, may hold values from 0.5 to 1.5
- w_out: bfloat16 [1024, 1024], P('row', 'col'), may hold values from -0.1875 to 0.1875
- norm_ffn: bfloat16 [1024], P('col'), may hold values from 0.5 to 1.5
- w_ffn_gate: bfloat16 [1024, 2816], P('col', 'row'), may hold values from -0.1875 to 0.1875
- w_ffn_up: bfloat16 [1024, 2816], P('col', 'row'), may hold values from -0.1875 to 0.1875
- w_ffn_down: bfloat16 [2816, 1024], P('row', 'col'), may hold values from -0.109375 to 0.109375
- segments: int32 [8, 1024], P(('dp', 'col')), may hold values from 0 to 2, never falling along the last dimension, each value on 1 to 512 neighbouring positions
- cotangent: bfloat16 [8192, 1024], P(('dp', 'row'), 'col'), may hold values from -6 to 6
Outputs:
- block_output: bfloat16 [8192, 1024], P(('dp', 'row'), 'col')
- grad_input: float32 [8192, 1024], P(('dp', 'row'), 'col')
- grad_norm_attn: float32 [1024], P('col')
- grad_w_query: float32 [1024, 512], P('col', 'row')
- grad_w_key: float32 [1024, 512], P('col', 'row')
- grad_w_value: float32 [1024, 1024], P('col', 'row')
- grad_w_gate_out: float32 [1024, 1024], P('col', 'row')
- grad_w_rank_in: float32 [1024, 16], P('col')
- grad_w_rank_out: float32 [16, 512], P(None, 'row')
- grad_rank_bias: float32 [512], P('row')
- grad_head_gain: float32 [256], replicated
- grad_w_out: float32 [1024, 1024], P('row', 'col')
- grad_norm_ffn: float32 [1024], P('col')
- grad_w_ffn_gate: float32 [1024, 2816], P('col', 'row')
- grad_w_ffn_up: float32 [1024, 2816], P('col', 'row')
- grad_w_ffn_down: float32 [2816, 1024], P('row', 'col')
The draws below stay inside these ranges and needn't reach their ends.
Inputs may be any that keep to these rules, and one draw needn't show every extreme that they name: `segments`: each row numbers the 3 documents of one packed sequence from 0 upward and never falls; every document has at least one token and at most 512, and one of each row has exactly 512. `w_query`: A projection with entries of standard deviation about 1024 ** -0.5. `w_key`: A projection with entries of standard deviation about 1024 ** -0.5.
All inputs are finite; a program needn't handle non-finite values.
Results may differ from the reference program's by a relative error of at most 0.02.
Values may be sent and summed in bfloat16 or wider, within the bound.
No kernel may reach another device: no remote copies, remote signals or barrier semaphores. Data moves between devices by JAX's collectives and lax.ppermute only.
A program may use at most 192 MiB of HBM per device.

```python
import math
from functools import partial
import jax
import jax.numpy as jnp
import numpy as np
from jax import lax

D = 1024
HEADS = 4
HEAD_K = 128
HEAD_V = 256
FF = 2816
RANK = 16
SPAN = 64
SEGS = 3
PACK = 1024
PACKS = 8
TOKENS = 8192


def query_key_pair(key):
    shape = (D, HEADS * HEAD_K)
    scale = D ** (-0.5)
    first = jnp.clip(jax.random.normal(jax.random.fold_in(key, 11), shape, jnp.float32), -5.0, 5.0) * scale
    other = jnp.clip(jax.random.normal(jax.random.fold_in(key, 23), shape, jnp.float32), -5.0, 5.0) * scale
    return (first, 0.8 * first + 0.6 * other)


def draw_w_query(key, part):
    first, second = query_key_pair(key)
    return first.astype(jnp.bfloat16)


def draw_w_key(key, part):
    first, second = query_key_pair(key)
    return second.astype(jnp.bfloat16)


def block_levels(stream_key, extent, cuts, low, top_value):
    factor_of, own = 1.0, jax.random.fold_in(stream_key, 6)
    for dim, blocks in cuts:
        steps = jnp.exp(jax.random.uniform(jax.random.fold_in(own, dim), (blocks,), jnp.float32, low / len(cuts), top_value / len(cuts)))
        factor_of = factor_of * jnp.repeat(steps, extent[dim] // blocks).reshape([-1 if axis == dim else 1 for axis in range(len(extent))])
    return factor_of


def profile(count, total, reach, skew):
    portions = [(1 << 20) // math.isqrt(grade ** skew) + 1 for grade in range(2, count + 1)]
    surplus, given = total - reach - (count - 1), [1] * (count - 1)
    while surplus > 0:
        movable = [i for i in range(count - 1) if given[i] < reach]
        mass, left = sum([portions[i] for i in movable]), surplus
        for i in movable:
            addition = min(reach - given[i], max(1, left * portions[i] // mass), surplus)
            given[i] = given[i] + addition
            surplus = surplus - addition
    return np.array([reach] + given)


def uneven(key, count, total, bound, skew):
    if count == 2:
        one = jax.random.randint(key, (), max(1, total - bound), min(bound, total - 1) + 1)
        return jnp.stack([one, total - one])
    tallies = jnp.asarray(profile(count, total, bound, skew), jnp.int32)
    pairs = (count - 1) // 2
    donor, receiver = tallies[1:1 + 2 * pairs:2], tallies[2:2 + 2 * pairs:2]
    margin = jnp.minimum(donor - 1, bound - receiver)
    passed = jax.random.randint(jax.random.fold_in(key, 1), (pairs,), 0, 1 << 20) % (margin + 1)
    tallies = tallies.at[1:1 + 2 * pairs:2].set(donor - passed).at[2:2 + 2 * pairs:2].set(receiver + passed)
    return tallies[jax.random.permutation(jax.random.fold_in(key, 2), count)]


def scatter_about(stream_key, dims, spread, bound, cuts=(), kind=jnp.bfloat16):
    array = spread * jax.random.normal(stream_key, dims, jnp.float32)
    if cuts:
        array = array * block_levels(stream_key, dims, cuts, -0.22, 0.18)
    return jnp.clip(array, -bound, bound).astype(kind)


def setup_inputs(seed: int = 0) -> dict:
    key_list = jax.random.split(jax.random.key(seed), 18)
    block_input = scatter_about(key_list[0], (TOKENS, D), 1.0, 6.0, ((0, 8), (1, 4)))
    norm_attn = jnp.clip(1.0 + 0.1 * jax.random.normal(key_list[1], (D,), jnp.float32), 0.5, 1.5).astype(jnp.bfloat16)
    w_query = draw_w_query(jax.random.fold_in(key_list[17], 71), 0)
    w_key = draw_w_key(jax.random.fold_in(key_list[17], 71), 0)
    w_value = scatter_about(key_list[4], (D, HEADS * HEAD_V), D ** -0.5, 0.1875, ((0, 4), (1, 4)))
    w_gate_out = scatter_about(key_list[5], (D, HEADS * HEAD_V), D ** -0.5, 0.1875, ((0, 4), (1, 4)))
    w_rank_in = scatter_about(key_list[6], (D, RANK), D ** -0.5, 0.1875, ((0, 4),))
    w_rank_out = scatter_about(key_list[7], (RANK, HEADS * HEAD_K), RANK ** -0.5, 1.5, ((1, 4),))
    rank_bias = jnp.clip(0.5 + 5.5 * jax.random.uniform(key_list[8], (HEADS * HEAD_K,), jnp.float32) ** block_levels(key_list[8], (HEADS * HEAD_K,), ((0, 4),), -0.2, 0.2), 0.5, 6.0).astype(jnp.bfloat16)
    head_gain = jnp.clip(1.0 + 0.1 * jax.random.normal(key_list[9], (HEAD_V,), jnp.float32), 0.5, 1.5).astype(jnp.bfloat16)
    w_out = scatter_about(key_list[10], (HEADS * HEAD_V, D), (HEADS * HEAD_V) ** -0.5, 0.1875, ((0, 4), (1, 4)))
    norm_ffn = jnp.clip(1.0 + 0.1 * jax.random.normal(key_list[11], (D,), jnp.float32), 0.5, 1.5).astype(jnp.bfloat16)
    w_ffn_gate = scatter_about(key_list[12], (D, FF), D ** -0.5, 0.1875, ((0, 4), (1, 4)))
    w_ffn_up = scatter_about(key_list[13], (D, FF), D ** -0.5, 0.1875, ((0, 4), (1, 4)))
    w_ffn_down = scatter_about(key_list[14], (FF, D), FF ** -0.5, 0.109375, ((0, 4), (1, 4)))
    segments = jax.vmap(lambda own: jnp.searchsorted(jnp.cumsum(uneven(own, SEGS, PACK, PACK // 2, 0)), jnp.arange(PACK), side="right"))(jax.random.split(key_list[15], PACKS)).reshape((PACKS, PACK)).astype(jnp.int32)
    cotangent = scatter_about(key_list[16], (TOKENS, D), 1.0, 6.0, ((0, 8), (1, 4)))
    return {"block_input": block_input, "norm_attn": norm_attn, "w_query": w_query, "w_key": w_key, "w_value": w_value, "w_gate_out": w_gate_out, "w_rank_in": w_rank_in, "w_rank_out": w_rank_out, "rank_bias": rank_bias, "head_gain": head_gain, "w_out": w_out, "norm_ffn": norm_ffn, "w_ffn_gate": w_ffn_gate, "w_ffn_up": w_ffn_up, "w_ffn_down": w_ffn_down, "segments": segments, "cotangent": cotangent}


@jax.custom_vjp
def low(v):
    return lax.optimization_barrier(v.astype(jnp.bfloat16)).astype(jnp.float32)

@jax.custom_vjp
def low_back(v):
    return v

def low_keep(v):
    return (low(v), None)

def low_pass(kept, grad):
    return (grad,)

def back_keep(v):
    return (v, None)

def back_low(kept, grad):
    return (low(grad),)
low.defvjp(low_keep, low_pass)
low_back.defvjp(back_keep, back_low)
norm_eps = 1e-06
head_eps = 1e-05
gate_scale = 16.0
exact_prec = lax.Precision.HIGHEST

def exact_dot(left_rows, right_rows):
    return jnp.dot(left_rows, right_rows, precision=exact_prec)

def rms_norm(values, gain_vec):
    return values * lax.rsqrt(lax.optimization_barrier(jnp.mean(values * values, axis=-1, keepdims=True)) + norm_eps) * gain_vec

def block_update(carried, pieces):
    state_kv, last_seg = carried
    query_c, key_c, value_c, decay_c, seg_c = pieces
    length = seg_c.shape[0]
    cumulative = jnp.cumsum(decay_c, axis=0)
    causal = jnp.arange(length)[:, None] >= jnp.arange(length)[None, :]
    allowed = jnp.logical_and(causal, seg_c[:, None] == seg_c[None, :])
    query_e = query_c * jnp.exp(cumulative)
    key_e = key_c * jnp.exp(-cumulative)
    scores = jnp.where(allowed, jnp.dot(query_e, key_e.T, precision=exact_prec), 0.0)
    from_state = jnp.where((seg_c == last_seg)[:, None], jnp.dot(query_e, state_kv, precision=exact_prec), 0.0)
    block_out = jnp.dot(scores, value_c, precision=exact_prec) + from_state
    final_seg = seg_c[length - 1].astype(jnp.int32)
    last_cum = cumulative[length - 1]
    key_d = jnp.where((seg_c == final_seg)[:, None], key_c * jnp.exp(last_cum[None, :] - cumulative), 0.0)
    keep_rate = jnp.where(final_seg == last_seg, jnp.exp(last_cum), 0.0)
    state_kv = state_kv * keep_rate[:, None] + jnp.dot(key_d.T, value_c, precision=exact_prec)
    return ((state_kv, final_seg), block_out)

def head_mix(head_proj, bias_vec, gain_vec, seg_row):
    seg_row = seg_row.astype(jnp.int32)
    query_part = head_proj[:, :HEAD_K] * HEAD_K ** (-0.5)
    key_part = head_proj[:, HEAD_K:2 * HEAD_K]
    value_part = head_proj[:, 2 * HEAD_K:2 * HEAD_K + HEAD_V]
    gate_part = head_proj[:, 2 * HEAD_K + HEAD_V:2 * HEAD_K + 2 * HEAD_V]
    logit_part = head_proj[:, 2 * HEAD_K + 2 * HEAD_V:] + bias_vec
    decay_part = jax.nn.log_sigmoid(logit_part) / gate_scale
    num_blocks = head_proj.shape[0] // SPAN

    def to_blocks(array_in):
        return array_in.reshape(num_blocks, SPAN, array_in.shape[-1])
    initial = (jnp.zeros((HEAD_K, HEAD_V), head_proj.dtype), jnp.int32(-1))
    unused, outs_all = lax.scan(jax.checkpoint(block_update), initial, (to_blocks(query_part), to_blocks(key_part), to_blocks(value_part), to_blocks(decay_part), seg_row.reshape(num_blocks, SPAN)))
    mixed_out = outs_all.reshape(-1, HEAD_V)
    normed = mixed_out * lax.rsqrt(lax.optimization_barrier(jnp.mean(mixed_out * mixed_out, axis=1, keepdims=True)) + head_eps) * gain_vec
    return normed * jax.nn.silu(gate_part)

def pack_mix(bias_vec, gain_vec, pair_args):
    return head_mix(pair_args[0], bias_vec, gain_vec, pair_args[1])

def forward(segments, block_input, norm_attn, w_query, w_key, w_value, w_gate_out, w_rank_in, w_rank_out, rank_bias, head_gain, w_out, norm_ffn, w_ffn_gate, w_ffn_up, w_ffn_down):
    normed_one = low(rms_norm(block_input, norm_attn))
    effective = low(exact_dot(w_rank_in, w_rank_out))
    proj_query = low_back(low(exact_dot(normed_one, w_query)))
    proj_key = low_back(low(exact_dot(normed_one, w_key)))
    proj_value = low_back(low(exact_dot(normed_one, w_value)))
    proj_gate = low_back(low(exact_dot(normed_one, w_gate_out)))
    proj_logit = low_back(low(exact_dot(normed_one, effective)))
    heads_out = []
    for head_index in range(HEADS):
        key_cols = slice(head_index * HEAD_K, (head_index + 1) * HEAD_K)
        value_cols = slice(head_index * HEAD_V, (head_index + 1) * HEAD_V)
        head_proj = jnp.concatenate([proj_query[:, key_cols], proj_key[:, key_cols], proj_value[:, value_cols], proj_gate[:, value_cols], proj_logit[:, key_cols]], axis=1)
        head_proj = head_proj.reshape(PACKS, PACK, head_proj.shape[1])
        mixed_out = lax.map(partial(pack_mix, rank_bias[key_cols], head_gain), (head_proj, segments.astype(jnp.int32)))
        heads_out.append(mixed_out.reshape(TOKENS, HEAD_V))
    gated_out = low(jnp.concatenate(heads_out, axis=1))
    attn_sum = low_back(exact_dot(gated_out, w_out))
    resid_mid = block_input + attn_sum
    normed_two = low(rms_norm(resid_mid, norm_ffn))
    gate_val = low_back(exact_dot(normed_two, w_ffn_gate))
    up_val = low_back(exact_dot(normed_two, w_ffn_up))
    hidden = low(jax.nn.silu(gate_val) * up_val)
    ffn_sum = low_back(exact_dot(hidden, w_ffn_down))
    return resid_mid + ffn_sum

def reference(block_input, norm_attn, w_query, w_key, w_value, w_gate_out, w_rank_in, w_rank_out, rank_bias, head_gain, w_out, norm_ffn, w_ffn_gate, w_ffn_up, w_ffn_down, segments, cotangent):
    as_float = jnp.float32
    result, pullback = jax.vjp(partial(forward, segments), block_input.astype(as_float), norm_attn.astype(as_float), w_query.astype(as_float), w_key.astype(as_float), w_value.astype(as_float), w_gate_out.astype(as_float), w_rank_in.astype(as_float), w_rank_out.astype(as_float), rank_bias.astype(as_float), head_gain.astype(as_float), w_out.astype(as_float), norm_ffn.astype(as_float), w_ffn_gate.astype(as_float), w_ffn_up.astype(as_float), w_ffn_down.astype(as_float))
    grads = pullback(cotangent.astype(as_float))
    return (result.astype(jnp.bfloat16), grads[0], grads[1], grads[2], grads[3], grads[4], grads[5], grads[6], grads[7], grads[8], grads[9], grads[10], grads[11], grads[12], grads[13], grads[14])
```

```python
from functools import partial

import jax
import jax.numpy as jnp
from jax import lax
from jax.experimental import pallas as pl
from jax.experimental.pallas import tpu as pltpu
from jax.sharding import PartitionSpec as P

D = 1024
HEAD_K = 128
HEAD_V = 256
SPAN = 64
norm_eps = 1e-06
head_eps = 1e-05
gate_scale = 16.0
exact_prec = lax.Precision.HIGHEST
f32 = jnp.float32
bf16 = jnp.bfloat16


def dot_nn(a, b):
    return lax.dot_general(a, b, (((1,), (0,)), ((), ())), preferred_element_type=f32)


def dot_nt(a, b):
    return lax.dot_general(a, b, (((1,), (1,)), ((), ())), preferred_element_type=f32)


def dot_tn(a, b):
    return lax.dot_general(a, b, (((0,), (0,)), ((), ())), preferred_element_type=f32)


def split_dot(ones_mat, values):
    hi = values.astype(bf16)
    rest = values - hi.astype(f32)
    mid = rest.astype(bf16)
    lo = (rest - mid.astype(f32)).astype(bf16)
    return dot_nn(ones_mat, hi) + (dot_nn(ones_mat, mid) + dot_nn(ones_mat, lo))


def common_parts(blk, proj_ref, logit_ref, bias_ref, segc_ref, segr_ref, block):
    scale = HEAD_K ** (-0.5)
    query = proj_ref[:, :HEAD_K].astype(f32) * scale
    key = proj_ref[:, HEAD_K : 2 * HEAD_K].astype(f32)
    value = proj_ref[:, 2 * HEAD_K : 2 * HEAD_K + HEAD_V]
    gate = proj_ref[:, 2 * HEAD_K + HEAD_V :].astype(f32)
    logit = logit_ref[...].astype(f32) + bias_ref[...]
    tail = jnp.exp(-jnp.abs(logit))
    decay = (jnp.minimum(logit, 0.0) - jnp.log1p(tail)) / gate_scale
    rows = lax.broadcasted_iota(jnp.int32, (blk, blk), 0)
    cols = lax.broadcasted_iota(jnp.int32, (blk, blk), 1)
    causal = jnp.logical_and(rows >= cols, rows // SPAN == cols // SPAN)
    tri = jnp.where(causal, 1.0, 0.0).astype(bf16)
    cumulative = split_dot(tri, decay)
    seg_col = segc_ref[...]
    seg_row = segr_ref[pl.ds(block, 1), :]
    same = jnp.broadcast_to(seg_col, (blk, blk)) == jnp.broadcast_to(seg_row, (blk, blk))
    allowed = jnp.logical_and(causal, same)
    return query, key, value, gate, logit, cumulative, seg_col, causal, allowed


def mix_forward_kernel(
    blk,
    key_s,
    seg_s,
    proj_ref,
    logit_ref,
    bias_ref,
    gain_ref,
    segc_ref,
    segr_ref,
    gated_ref,
    mixed_ref,
    states_ref,
    state,
):
    block = pl.program_id(0)

    @pl.when(block == 0)
    def _():
        state[...] = jnp.zeros_like(state)

    query, key, value, gate, logit, cum, seg_col, causal, allowed = common_parts(
        blk, proj_ref, logit_ref, bias_ref, segc_ref, segr_ref, block
    )
    query_e = (query * jnp.exp(cum)).astype(bf16)
    key_e = (key * jnp.exp(-cum)).astype(bf16)
    scores = jnp.where(allowed, dot_nt(query_e, key_e), 0.0).astype(bf16)
    inner = dot_nn(scores, value)
    carried = state[...]
    pieces = []
    for n in range(blk // SPAN):
        part = slice(n * SPAN, (n + 1) * SPAN)
        base = block * blk + n * SPAN
        last_seg = jnp.where(base > 0, seg_s[jnp.maximum(base - 1, 0)], -1)
        final_seg = seg_s[base + SPAN - 1]
        states_ref[n] = carried
        seg_v = jnp.broadcast_to(seg_col[part], (SPAN, HEAD_V))
        seg_k = jnp.broadcast_to(seg_col[part], (SPAN, HEAD_K))
        from_state = jnp.where(
            seg_v == last_seg, dot_nt(query_e[part], carried.astype(bf16)), 0.0
        )
        last_cum = cum[(n + 1) * SPAN - 1 : (n + 1) * SPAN, :]
        key_d = jnp.where(seg_k == final_seg, key[part] * jnp.exp(last_cum - cum[part]), 0.0)
        keep = jnp.where(final_seg == last_seg, jnp.exp(last_cum), 0.0)
        carried = carried * keep + dot_tn(value[part], key_d.astype(bf16))
        pieces.append(inner[part] + from_state)
    state[...] = carried
    mixed = jnp.concatenate(pieces, axis=0)
    mixed_ref[...] = mixed
    inv = lax.rsqrt(jnp.mean(mixed * mixed, axis=1, keepdims=True) + head_eps)
    silu = gate / (1.0 + jnp.exp(-gate))
    gated_ref[...] = (mixed * inv * gain_ref[...] * silu).astype(bf16)


def mix_backward_kernel(
    blk,
    blocks,
    key_s,
    seg_s,
    proj_ref,
    logit_ref,
    bias_ref,
    gain_ref,
    segc_ref,
    segr_ref,
    mixed_ref,
    states_ref,
    grad_ref,
    dproj_ref,
    dlogit_ref,
    dbias_ref,
    dgain_ref,
    dstate,
):
    step = pl.program_id(0)
    block = blocks - 1 - step

    @pl.when(step == 0)
    def _():
        dstate[...] = jnp.zeros_like(dstate)
        dbias_ref[...] = jnp.zeros_like(dbias_ref)
        dgain_ref[...] = jnp.zeros_like(dgain_ref)

    query, key, value, gate, logit, cum, seg_col, causal, allowed = common_parts(
        blk, proj_ref, logit_ref, bias_ref, segc_ref, segr_ref, block
    )
    mixed = mixed_ref[...]
    grad = grad_ref[...]
    gain = gain_ref[...]
    inv = lax.rsqrt(jnp.mean(mixed * mixed, axis=1, keepdims=True) + head_eps)
    sig = 1.0 / (1.0 + jnp.exp(-gate))
    silu = gate * sig
    normed = mixed * inv
    grad_norm = grad * normed
    dgain_ref[...] += jnp.sum(grad_norm * silu, axis=0, keepdims=True)
    dgate = grad_norm * gain * sig * (1.0 + gate * (1.0 - sig))
    weighted = grad * gain * silu
    inner = jnp.mean(weighted * mixed, axis=1, keepdims=True)
    dmixed = inv * weighted - mixed * (inv * inv * inv) * inner
    grow = jnp.exp(cum)
    shrink = jnp.exp(-cum)
    query_e = query * grow
    key_e = key * shrink
    query_b = query_e.astype(bf16)
    key_b = key_e.astype(bf16)
    dmixed_b = dmixed.astype(bf16)
    scores = jnp.where(allowed, dot_nt(query_b, key_b), 0.0).astype(bf16)
    dscores = jnp.where(allowed, dot_nt(dmixed_b, value), 0.0).astype(bf16)
    dvalue_in = dot_tn(scores, dmixed_b)
    dquery_in = dot_nn(dscores, key_b)
    dkey_in = dot_tn(dscores, query_b)
    carried = dstate[...]
    chunks = blk // SPAN
    dq_parts, dk_parts, dv_parts, dc_parts = [], [], [], []
    sub = lax.broadcasted_iota(jnp.int32, (SPAN, HEAD_K), 0)
    for n in reversed(range(chunks)):
        part = slice(n * SPAN, (n + 1) * SPAN)
        base = block * blk + n * SPAN
        last_seg = jnp.where(base > 0, seg_s[jnp.maximum(base - 1, 0)], -1)
        final_seg = seg_s[base + SPAN - 1]
        before = states_ref[n]
        seg_v = jnp.broadcast_to(seg_col[part], (SPAN, HEAD_V))
        seg_k = jnp.broadcast_to(seg_col[part], (SPAN, HEAD_K))
        last_cum = cum[(n + 1) * SPAN - 1 : (n + 1) * SPAN, :]
        fade = jnp.where(seg_k == final_seg, jnp.exp(last_cum - cum[part]), 0.0)
        key_d = key[part] * fade
        keep = jnp.where(final_seg == last_seg, jnp.exp(last_cum), 0.0)
        carried_b = carried.astype(bf16)
        dout_s = jnp.where(seg_v == last_seg, dmixed[part], 0.0).astype(bf16)
        dquery_e = dquery_in[part] + dot_nn(dout_s, before.astype(bf16))
        dkey_d = dot_nn(value[part], carried_b)
        dvalue = dvalue_in[part] + dot_nt(key_d.astype(bf16), carried_b)
        dkeep = jnp.sum(carried * before, axis=0, keepdims=True)
        from_key = dkey_d * key_d
        dlast = keep * dkeep + jnp.sum(from_key, axis=0, keepdims=True)
        carried = carried * keep + dot_tn(dout_s, query_b[part])
        dkey_e = dkey_in[part]
        dcum = dquery_e * query_e[part] - dkey_e * key_e[part] - from_key
        dcum = dcum + jnp.where(sub == SPAN - 1, jnp.broadcast_to(dlast, (SPAN, HEAD_K)), 0.0)
        dq_parts.append(dquery_e * grow[part])
        dk_parts.append(dkey_e * shrink[part] + dkey_d * fade)
        dv_parts.append(dvalue)
        dc_parts.append(dcum)
    dstate[...] = carried
    dcum = jnp.concatenate(dc_parts[::-1], axis=0)
    rows = lax.broadcasted_iota(jnp.int32, (blk, blk), 0)
    cols = lax.broadcasted_iota(jnp.int32, (blk, blk), 1)
    later = jnp.logical_and(rows <= cols, rows // SPAN == cols // SPAN)
    upper = jnp.where(later, 1.0, 0.0).astype(bf16)
    ddecay = split_dot(upper, dcum)
    dlogit = ddecay / gate_scale * (1.0 / (1.0 + jnp.exp(logit)))
    scale = HEAD_K ** (-0.5)
    dproj_ref[:, :HEAD_K] = (jnp.concatenate(dq_parts[::-1], axis=0) * scale).astype(bf16)
    dproj_ref[:, HEAD_K : 2 * HEAD_K] = jnp.concatenate(dk_parts[::-1], axis=0).astype(bf16)
    dproj_ref[:, 2 * HEAD_K : 2 * HEAD_K + HEAD_V] = jnp.concatenate(
        dv_parts[::-1], axis=0
    ).astype(bf16)
    dproj_ref[:, 2 * HEAD_K + HEAD_V :] = dgate.astype(bf16)
    dlogit_ref[...] = dlogit.astype(bf16)
    dbias_ref[...] += jnp.sum(dlogit, axis=0, keepdims=True)


def mix_specs(blk, blocks, place):
    wide = 2 * HEAD_K + 2 * HEAD_V
    return [
        pl.BlockSpec((blk, wide), place),
        pl.BlockSpec((blk, HEAD_K), place),
        pl.BlockSpec((1, HEAD_K), lambda i, key, seg: (0, 0)),
        pl.BlockSpec((1, HEAD_V), lambda i, key, seg: (0, 0)),
    ]


def mix_forward(order_key, seg, proj, logit, bias, gain, blocks):
    tokens = proj.shape[0]
    blk = tokens // blocks
    chunks = blk // SPAN

    def place(i, key, seg):
        return (jnp.bitwise_xor(i, key[0]), 0)

    return pl.pallas_call(
        partial(mix_forward_kernel, blk),
        grid_spec=pltpu.PrefetchScalarGridSpec(
            num_scalar_prefetch=2,
            grid=(blocks,),
            in_specs=mix_specs(blk, blocks, place)
            + [
                pl.BlockSpec((blk, 1), lambda i, key, seg: (i, 0)),
                pl.BlockSpec((blocks, blk), lambda i, key, seg: (0, 0)),
            ],
            out_specs=[
                pl.BlockSpec((blk, HEAD_V), place),
                pl.BlockSpec((blk, HEAD_V), place),
                pl.BlockSpec((chunks, HEAD_V, HEAD_K), lambda i, key, seg: (i, 0, 0)),
            ],
            scratch_shapes=[pltpu.VMEM((HEAD_V, HEAD_K), f32)],
        ),
        out_shape=[
            jax.ShapeDtypeStruct((tokens, HEAD_V), bf16),
            jax.ShapeDtypeStruct((tokens, HEAD_V), f32),
            jax.ShapeDtypeStruct((tokens // SPAN, HEAD_V, HEAD_K), f32),
        ],
        cost_estimate=pl.CostEstimate(
            flops=tokens * 1000000, bytes_accessed=tokens * 8000, transcendentals=tokens * 1000
        ),
        name="mix_forward",
    )(order_key, seg, proj, logit, bias, gain, seg.reshape(tokens, 1), seg.reshape(blocks, blk))


def mix_backward(order_key, seg, proj, logit, bias, gain, mixed, states, grad, blocks):
    tokens = proj.shape[0]
    blk = tokens // blocks
    chunks = blk // SPAN
    wide = 2 * HEAD_K + 2 * HEAD_V

    def place(i, key, seg):
        return (jnp.bitwise_xor(blocks - 1 - i, key[0]), 0)

    return pl.pallas_call(
        partial(mix_backward_kernel, blk, blocks),
        grid_spec=pltpu.PrefetchScalarGridSpec(
            num_scalar_prefetch=2,
            grid=(blocks,),
            in_specs=mix_specs(blk, blocks, place)
            + [
                pl.BlockSpec((blk, 1), lambda i, key, seg: (blocks - 1 - i, 0)),
                pl.BlockSpec((blocks, blk), lambda i, key, seg: (0, 0)),
                pl.BlockSpec((blk, HEAD_V), place),
                pl.BlockSpec(
                    (chunks, HEAD_V, HEAD_K), lambda i, key, seg: (blocks - 1 - i, 0, 0)
                ),
                pl.BlockSpec((blk, HEAD_V), place),
            ],
            out_specs=[
                pl.BlockSpec((blk, wide), place),
                pl.BlockSpec((blk, HEAD_K), place),
                pl.BlockSpec((1, HEAD_K), lambda i, key, seg: (0, 0)),
                pl.BlockSpec((1, HEAD_V), lambda i, key, seg: (0, 0)),
            ],
            scratch_shapes=[pltpu.VMEM((HEAD_V, HEAD_K), f32)],
        ),
        out_shape=[
            jax.ShapeDtypeStruct((tokens, wide), bf16),
            jax.ShapeDtypeStruct((tokens, HEAD_K), bf16),
            jax.ShapeDtypeStruct((1, HEAD_K), f32),
            jax.ShapeDtypeStruct((1, HEAD_V), f32),
        ],
        cost_estimate=pl.CostEstimate(
            flops=tokens * 2000000, bytes_accessed=tokens * 12000, transcendentals=tokens * 1500
        ),
        name="mix_backward",
    )(
        order_key,
        seg,
        proj,
        logit,
        bias,
        gain,
        seg.reshape(tokens, 1),
        seg.reshape(blocks, blk),
        mixed,
        states,
        grad,
    )


def swap_plan(rows, cols):
    per_row = cols // rows
    plan = []
    for k in range(cols):
        pairs = []
        for r in range(rows):
            for c in range(cols):
                m = (c + k) % cols
                pairs.append((r * cols + c, (m % rows) * cols + r * per_row + m // rows))
        plan.append(pairs)
    return plan


def to_working(values, rows, cols):
    col = lax.axis_index("col")
    row = lax.axis_index("row")
    size = values.shape[0] // cols
    width = values.shape[1]
    parts = []
    for k, pairs in enumerate(swap_plan(rows, cols)):
        m = (col + k) % cols
        block = lax.dynamic_slice_in_dim(values, m * size, size, axis=0)
        parts.append(lax.ppermute(block, ("row", "col"), pairs))
    mine = (col % (cols // rows)) * rows + row
    turned = parts[::-1]
    start = (2 * cols - 1 - mine) % cols
    doubled = jnp.concatenate(turned + turned[:-1], axis=1)
    return lax.dynamic_slice_in_dim(doubled, start * width, cols * width, axis=1)


def to_given(values, rows, cols):
    col = lax.axis_index("col")
    row = lax.axis_index("row")
    width = values.shape[1] // cols
    size = values.shape[0]
    mine = (col % (cols // rows)) * rows + row
    parts = []
    for k, pairs in enumerate(swap_plan(rows, cols)):
        c = (mine - k + cols) % cols
        block = lax.dynamic_slice_in_dim(values, c * width, width, axis=1)
        back = [(dst, src) for src, dst in pairs]
        parts.append(lax.ppermute(block, ("row", "col"), back))
    start = (cols - col) % cols
    doubled = jnp.concatenate(parts + parts[:-1], axis=0)
    return lax.dynamic_slice_in_dim(doubled, start * size, cols * size, axis=0)


def flip(values, bit, count):
    return lax.ppermute(values, "row", [(i, i ^ bit) for i in range(count)])


def gather_rows(part, rows):
    if rows != 4:
        return lax.all_gather(part, "row", axis=0, tiled=True)
    near = flip(part, 1, rows)
    far = flip(part, 2, rows)
    other = flip(far, 1, rows)
    return jnp.concatenate([part, near, far, other], axis=0)


def reduce_rows(terms, rows):
    if rows != 4:
        return lax.psum_scatter(
            terms.astype(bf16), "row", scatter_dimension=0, tiled=True
        ).astype(f32)
    size = terms.shape[0] // rows
    piece = [terms[j * size : (j + 1) * size] for j in range(rows)]
    got_far = flip(piece[3].astype(bf16), 1, rows).astype(f32)
    got_near = flip(piece[1].astype(bf16), 1, rows).astype(f32)
    got = flip((piece[2] + got_far).astype(bf16), 2, rows).astype(f32)
    return piece[0] + got_near + got


def reduce_weight(terms, dps):
    part = lax.psum_scatter(terms.astype(bf16), "col", scatter_dimension=0, tiled=True)
    if dps == 2:
        other = lax.ppermute(part, "dp", [(0, 1), (1, 0)])
        return part.astype(f32) + other.astype(f32)
    return lax.psum(part.astype(f32), "dp")


def gather_weight(part):
    return lax.all_gather(part, "col", axis=0, tiled=True)


def rms_forward(values, gain_vec):
    inv_rms = lax.rsqrt(jnp.mean(values * values, axis=1, keepdims=True) + norm_eps)
    return (values * inv_rms * gain_vec, inv_rms)


def rms_backward(values, inv_rms, gain_vec, grad_normed):
    weighted = grad_normed * gain_vec
    inner = jnp.mean(weighted * values, axis=1, keepdims=True)
    grad_values = inv_rms * weighted - values * (inv_rms * inv_rms * inv_rms) * inner
    grad_gain = jnp.sum(grad_normed * values * inv_rms, axis=0)
    return (grad_values, grad_gain)


def local(
    rows,
    cols,
    dps,
    block_input,
    norm_attn,
    w_query,
    w_key,
    w_value,
    w_gate_out,
    w_rank_in,
    w_rank_out,
    rank_bias,
    head_gain,
    w_out,
    norm_ffn,
    w_ffn_gate,
    w_ffn_up,
    w_ffn_down,
    segments,
    cotangent,
):
    row = lax.axis_index("row")
    col = lax.axis_index("col")
    rank = w_rank_in.shape[1]
    ffn_width = w_ffn_gate.shape[1]
    features = block_input.shape[1]
    mix_width = 2 * HEAD_K + 2 * HEAD_V
    order_key = (row if rows == 4 else jnp.int32(0)).reshape(1).astype(jnp.int32)

    gains = jnp.concatenate([norm_attn[:, None], norm_ffn[:, None]], axis=1)
    first = gather_weight(
        jnp.concatenate([w_query, w_key, w_value, w_gate_out, w_rank_in, gains], axis=1)
    )
    w_mix = first[:, :mix_width]
    rank_in_all = first[:, mix_width : mix_width + rank]
    gain_attn = first[:, mix_width + rank].astype(f32)[None, :]
    gain_ffn = first[:, mix_width + rank + 1].astype(f32)[None, :]
    effective = jnp.dot(rank_in_all, w_rank_out, preferred_element_type=f32).astype(bf16)
    w_out_t = gather_weight(w_out.T)
    w_pair = gather_weight(jnp.concatenate([w_ffn_gate, w_ffn_up], axis=1))
    w_down_t = gather_weight(w_ffn_down.T)

    tokens_in = to_working(block_input, rows, cols).astype(f32)
    normed_one, scale_one = rms_forward(tokens_in, gain_attn)
    rows_one = gather_rows(normed_one.astype(bf16), rows)
    proj = dot_nn(rows_one, w_mix).astype(bf16)
    logit = dot_nn(rows_one, effective).astype(bf16)
    bias_row = rank_bias.astype(f32)[None, :]
    gain_row = head_gain.astype(f32)[None, :]
    seg = segments.reshape(-1)
    gated, mixed, states = mix_forward(
        order_key, seg, proj, logit, bias_row, gain_row, rows
    )
    resid_mid = tokens_in + reduce_rows(dot_nt(gated, w_out_t), rows)
    normed_two, scale_two = rms_forward(resid_mid, gain_ffn)
    rows_two = gather_rows(normed_two.astype(bf16), rows)
    cot_part = to_working(cotangent, rows, cols)
    rows_cot = gather_rows(cot_part, rows)
    gate_up = dot_nn(rows_two, w_pair)
    gate_val = gate_up[:, :ffn_width]
    up_val = gate_up[:, ffn_width:]
    gate_sig = jax.nn.sigmoid(gate_val)
    hidden = (gate_val * gate_sig * up_val).astype(bf16)
    grad_hidden = dot_nn(rows_cot, w_down_t)
    grad_gate = grad_hidden * up_val * gate_sig * (1.0 + gate_val * (1.0 - gate_sig))
    grad_up = grad_hidden * gate_val * gate_sig
    grad_pairs = jnp.concatenate([grad_gate, grad_up], axis=1).astype(bf16)
    grad_normed_two = reduce_rows(dot_nt(grad_pairs, w_pair), rows)
    grad_two, gain_two = rms_backward(resid_mid, scale_two, gain_ffn, grad_normed_two)
    grad_mid = cot_part.astype(f32) + grad_two
    rows_mid = gather_rows(grad_mid.astype(bf16), rows)
    block_out = resid_mid + reduce_rows(dot_nt(hidden, w_down_t), rows)
    block_out = to_given(block_out.astype(bf16), rows, cols)
    grad_gated = dot_nn(rows_mid, w_out_t)
    grad_pair_w = reduce_weight(dot_tn(rows_two, grad_pairs), dps)
    grad_down_w = reduce_weight(dot_tn(rows_cot, hidden), dps).T
    dproj, dlogit, dbias, dgain = mix_backward(
        order_key, seg, proj, logit, bias_row, gain_row, mixed, states, grad_gated, rows
    )
    grad_out_w = reduce_weight(dot_tn(rows_mid, gated), dps).T
    grad_normed_one = reduce_rows(dot_nt(dproj, w_mix) + dot_nt(dlogit, effective), rows)
    grad_one, gain_one = rms_backward(tokens_in, scale_one, gain_attn, grad_normed_one)
    grad_input = to_given((grad_one + grad_mid).astype(bf16), rows, cols).astype(f32)
    grad_mix_w = reduce_weight(dot_tn(rows_one, dproj), dps)
    grad_eff = dot_tn(rows_one, dlogit)
    rank_in_part = jnp.dot(grad_eff, w_rank_out.astype(f32).T, precision=exact_prec)
    rank_out_part = jnp.dot(rank_in_all.astype(f32).T, grad_eff, precision=exact_prec)

    own = jnp.concatenate([rank_out_part.reshape(-1), dbias.reshape(-1)])
    slots = jnp.where(jnp.arange(rows)[:, None] == row, own[None, :], 0.0)
    small = jnp.concatenate(
        [rank_in_part.reshape(-1), dgain.reshape(-1), gain_two, slots.reshape(-1)]
    )
    small = lax.psum(small, ("dp", "row", "col"))
    gain_one = lax.psum(gain_one, ("dp", "row", "col"))
    full = cols * features
    rank_in_all_g = small[: full * rank].reshape(full, rank)
    grad_rank_in = lax.dynamic_slice_in_dim(rank_in_all_g, col * features, features, axis=0)
    at = full * rank
    grad_head_gain = small[at : at + HEAD_V]
    at += HEAD_V
    gain_two = lax.dynamic_slice_in_dim(small[at : at + full], col * features, features)
    at += full
    own = lax.dynamic_index_in_dim(small[at:].reshape(rows, -1), row, 0, keepdims=False)
    grad_rank_out = own[: rank * HEAD_K].reshape(rank, HEAD_K)
    grad_bias = own[rank * HEAD_K :]
    gain_one = lax.dynamic_slice_in_dim(gain_one, col * features, features)
    return (
        block_out,
        grad_input,
        gain_one,
        grad_mix_w[:, :HEAD_K],
        grad_mix_w[:, HEAD_K : 2 * HEAD_K],
        grad_mix_w[:, 2 * HEAD_K : 2 * HEAD_K + HEAD_V],
        grad_mix_w[:, 2 * HEAD_K + HEAD_V :],
        grad_rank_in,
        grad_rank_out,
        grad_bias,
        grad_head_gain,
        grad_out_w,
        gain_two,
        grad_pair_w[:, :ffn_width],
        grad_pair_w[:, ffn_width:],
        grad_down_w,
    )


def solution(mesh):
    tokens = P(("dp", "row"), "col")
    inner = P("col", "row")
    outer = P("row", "col")
    in_specs = (
        tokens, P("col"), inner, inner, inner, inner, P("col", None), P(None, "row"),
        P("row"), P(), outer, P("col"), inner, inner, outer, P(("dp", "col"), None), tokens,
    )
    out_specs = (
        tokens, tokens, P("col"), inner, inner, inner, inner, P("col", None), P(None, "row"),
        P("row"), P(), outer, P("col"), inner, inner, outer,
    )
    step = partial(local, mesh.shape["row"], mesh.shape["col"], mesh.shape["dp"])
    return jax.shard_map(step, mesh=mesh, in_specs=in_specs, out_specs=out_specs, check_vma=False)
```
